256 devices in a mesh: pair: 2 (over x_hi), blk: 32 (over x_lo, z, core), rows: 4 (over y).
Axes of the slice: x: 4 (x_hi: 2, x_lo: 2; x = x_hi * 2 + x_lo), y: 4, z: 8, core: 2. Of those that a mesh axis runs over, the one named last changes fastest.
Arguments:
- tiles: float32 [2, 2048, 131072], P('pair', None, ('blk', 'rows')), may hold values from -0.0625 to 0.0625
- trial: float32 [2, 131072, 1024], P('pair', ('blk', 'rows')), may hold values from -6 to 6
Outputs:
- products: float32 [2, 2048, 1024], P('pair', ('blk', 'rows'))
The draws below stay inside these ranges and needn't reach their ends.
All inputs are finite; a program needn't handle non-finite values.
Results may differ from the reference program's by a relative error of at most 0.000076.
Values sent between devices are 32-bit elements; how exact they have to be, the bound alone decides.
A program may use at most 128 MiB of HBM per device.

```python
import jax
import jax.numpy as jnp
from jax import lax

N = 131072
W = 2048
K = 1024


def spiked(drawn, own_key, source, target, blocks, factor):
    owner, partner = [(jnp.arange(drawn.shape[dim]) // (drawn.shape[dim] // blocks)).reshape([-1 if axis == dim else 1 for axis in range(drawn.ndim)]) for dim in (source, target)]
    chosen = jax.random.permutation(own_key, blocks)[partner]
    strong = (owner == chosen) | (owner == (partner + blocks // 2) % blocks)
    return jnp.where(strong, factor * drawn, drawn)


def block_scale(key, extent, pieces, low, high):
    loudness, own = 1.0, jax.random.fold_in(key, 6)
    for position, shards_of in pieces:
        heights = jnp.exp(jax.random.uniform(jax.random.fold_in(own, position), (shards_of,), jnp.float32, low / len(pieces), high / len(pieces)))
        loudness = loudness * jnp.repeat(heights, extent[position] // shards_of).reshape([-1 if axis == position else 1 for axis in range(len(extent))])
    return loudness


def centred(key, shape, spread, bound, pieces=(), held_as=jnp.bfloat16):
    result = spread * jax.random.normal(key, shape, jnp.float32)
    if pieces:
        result = result * block_scale(key, shape, pieces, -0.22, 0.18)
    return jnp.clip(result, -bound, bound).astype(held_as)


def noise_with(rng, dims, scale, limit, split, heavy, kind=jnp.bfloat16):
    result = scale * jax.random.normal(rng, dims, jnp.float32)
    if split:
        result = result * block_scale(rng, dims, split, -0.22, 0.18)
    return jnp.clip(spiked(result, jax.random.fold_in(rng, 3), *heavy), -limit, limit).astype(kind)


def setup_inputs(seed: int = 0) -> dict:
    keys = jax.random.split(jax.random.key(seed), 3)
    return {
        "tiles": noise_with(keys[0], (2, W, N), N ** -0.5, 0.0625, ((0, 2), (2, 128)), (2, 1, 128, 5.5), jnp.float32),
        "trial": centred(keys[1], (2, N, K), 1.0, 6.0, ((0, 2), (1, 128)), jnp.float32),
    }


def reference(tiles, trial):
    sum_vectors = trial[0] + trial[1]
    diff_vectors = trial[0] - trial[1]
    plus_products = jnp.dot(tiles[0], sum_vectors, precision=lax.Precision.HIGHEST, preferred_element_type=jnp.float32)
    minus_products = jnp.dot(tiles[1], diff_vectors, precision=lax.Precision.HIGHEST, preferred_element_type=jnp.float32)
    upper_half = 0.5 * (plus_products + minus_products)
    lower_half = 0.5 * (plus_products - minus_products)
    return jnp.stack([upper_half, lower_half])
```

```python
import functools

import jax
import jax.numpy as jnp
from jax import lax
from jax.experimental import pallas as pl
from jax.experimental.pallas import tpu as pltpu
from jax.sharding import Mesh
from jax.sharding import PartitionSpec as P

MESH = pl.DeviceIdType.MESH
AXES = ("pair", "xlo", "z", "core", "y")
OWNERS = ("xlo", "z", "core", "y")
LANES = 128
ROWS_AT_ONCE = 512
STAGED = 256


def kernel(
    n_z, n_y, rows, relay,
    a_hbm, x_hbm, out_ref,
    xv, yv, passing, a_hi, a_lo, staged, b_parts,
    prod, core_in, y_in, s2, z_in, s3, far_in,
    x_sem, a_sem, own_send, pass_recv, fwd_send, fwd_recv,
    core_send, core_recv, y_send, y_recv, z_send, z_recv, far_send, far_recv,
):
    p, xlo, z, core, y = (lax.axis_index(a) for a in AXES)
    chunks = xv.shape[0]
    depth, width = a_hbm.shape[1], a_hbm.shape[0]
    half = depth // 2
    x_at = 2 * p + xlo
    sign = 1.0 - 2.0 * p.astype(jnp.float32)

    def along_x(step):
        there = lax.rem(x_at + step + 4, 4)
        return {"pair": there // 2, "xlo": lax.rem(there, 2)}

    right, left = along_x(1), along_x(-1)
    partner = {"pair": 1 - p}
    sibling = {"core": 1 - core}
    y_peers = [{"y": lax.rem(y + d, n_y)} for d in range(1, n_y)]
    z_peers = [{"z": lax.rem(z + d, n_z)} for d in range(1, n_z)]
    far_peers = [
        {"xlo": 1 - xlo},
        {"pair": 1 - p},
        {"pair": 1 - p, "xlo": 1 - xlo},
    ]
    peers = [sibling, *y_peers, *z_peers, *far_peers]

    barrier = pltpu.get_barrier_semaphore()
    for peer in peers:
        pl.semaphore_signal(barrier, inc=1, device_id=peer, device_id_type=MESH)

    def columns(j):
        return pl.ds(pl.multiple_of(j * LANES, LANES), LANES)

    def x_load(j):
        return pltpu.make_async_copy(x_hbm.at[:, columns(j)], xv.at[j], x_sem.at[j])

    def a_load(i):
        slot = lax.rem(i, 2)
        return pltpu.make_async_copy(
            a_hbm.at[pl.ds(pl.multiple_of(i * STAGED, STAGED), STAGED)], staged.at[slot], a_sem.at[slot]
        )

    def remote(src, dst, send, recv, peer):
        return pltpu.make_async_remote_copy(
            src_ref=src, dst_ref=dst, send_sem=send, recv_sem=recv, device_id=peer, device_id_type=MESH
        )

    ways = ((0, right), (1, left))

    def own(j, way, peer):
        return remote(
            x_hbm.at[pl.ds(way * half, half), columns(j)],
            passing.at[j, way],
            own_send.at[j, way],
            pass_recv.at[j, way],
            peer,
        )

    def forward(j, way, peer):
        return remote(
            passing.at[j, way],
            yv.at[j, pl.ds(way * half, half)],
            fwd_send.at[j, way],
            fwd_recv.at[j, way],
            peer,
        )

    def direct(j):
        return remote(x_hbm.at[:, columns(j)], yv.at[j], fwd_send.at[j, 0], fwd_recv.at[j, 0], partner)

    a_load(0).start()
    a_load(1).start()
    pl.semaphore_wait(barrier, len(peers))

    if relay:
        for j in range(2):
            for way, peer in ways:
                own(j, way, peer).start()
    else:
        for j in range(chunks):
            direct(j).start()

    def start_x(j, _):
        x_load(j).start()
        return 0

    lax.fori_loop(0, chunks, start_x, 0)

    pieces = width // STAGED

    def split_a(i, _):
        a_load(i).wait()
        slot = lax.rem(i, 2)
        here = pl.ds(pl.multiple_of(i * STAGED, STAGED), STAGED)
        value = staged[slot]
        high = value.astype(jnp.bfloat16)
        a_hi[here] = high
        a_lo[here] = (value - high.astype(jnp.float32)).astype(jnp.bfloat16)

        @pl.when(i + 2 < pieces)
        def _():
            a_load(i + 2).start()

        return 0

    lax.fori_loop(0, pieces, split_a, 0)

    def core_copy(j, first, count):
        return remote(
            prod.at[j, pl.ds(first, count), 1 - core],
            core_in.at[j, pl.ds(first, count)],
            core_send.at[j],
            core_recv.at[j],
            sibling,
        )

    groups = prod.shape[1]
    step_groups = ROWS_AT_ONCE // LANES

    def relay_step(j):
        for way, peer in ways:
            own(j, way, peer).wait_recv()
            forward(j, way, peer).start()

        @pl.when(j + 2 < chunks)
        def _():
            for way, peer in ways:
                own(j + 2, way, peer).start()

    def multiply(j):
        x_load(j).wait()
        if relay:
            for way, peer in ways:
                forward(j, way, peer).wait_recv()
        else:
            direct(j).wait_recv()
        combined = yv[j] + sign * xv[j]
        high = combined.astype(jnp.bfloat16)
        b_parts[:, :LANES] = high
        b_parts[:, LANES:] = (combined - high.astype(jnp.float32)).astype(jnp.bfloat16)

        def rows_step(m, _):
            here = pl.ds(pl.multiple_of(m * ROWS_AT_ONCE, ROWS_AT_ONCE), ROWS_AT_ONCE)
            main = jnp.dot(a_hi[here], b_parts[...], preferred_element_type=jnp.float32)
            rest = jnp.dot(a_lo[here], b_parts[:, :LANES], preferred_element_type=jnp.float32)
            total = main[:, :LANES] + (main[:, LANES:] + rest)
            first = m * step_groups
            prod[j, pl.ds(first, step_groups)] = total.reshape(step_groups, 2, n_y, rows, LANES)
            core_copy(j, first, step_groups).start()
            return 0

        lax.fori_loop(0, width // ROWS_AT_ONCE, rows_step, 0)

    def y_copy(j, d):
        return remote(
            prod.at[j, :, core, lax.rem(y + d, n_y)], y_in.at[j, n_y - 1 - d], y_send.at[j], y_recv.at[j], y_peers[d - 1]
        )

    def y_all(j):
        return remote(y_in.at[j], y_in.at[j], y_send.at[j], y_recv.at[j], y_peers[0])

    def z_copy(j, d):
        return remote(
            s2.at[j, :, lax.rem(z + d, n_z)], z_in.at[j, n_z - 1 - d], z_send.at[j], z_recv.at[j], z_peers[d - 1]
        )

    def z_all(j):
        return remote(z_in.at[j], z_in.at[j], z_send.at[j], z_recv.at[j], z_peers[0])

    def far_copy(j, k):
        column = 1 - xlo if k != 1 else xlo
        return remote(s3.at[j, column], far_in.at[j, k], far_send.at[j], far_recv.at[j], far_peers[k])

    def far_all(j):
        return remote(far_in.at[j], far_in.at[j], far_send.at[j], far_recv.at[j], far_peers[0])

    def after_core(j):
        core_copy(j, 0, groups).wait_recv()
        prod[j, :, core] = prod[j, :, core] + core_in[j]
        for d in range(1, n_y):
            y_copy(j, d).start()

    def after_y(j):
        y_all(j).wait_recv()
        total = prod[j, :, core, y]
        for d in range(n_y - 1):
            total = total + y_in[j, d]
        s2[j] = total.reshape(s2.shape[1:])
        for d in range(1, n_z):
            z_copy(j, d).start()

    def after_z(j):
        z_all(j).wait_recv()
        total = s2[j, :, z]
        for d in range(n_z - 1):
            total = total + z_in[j, d]
        s3[j] = total
        for k in range(3):
            far_copy(j, k).start()

    def after_far(j):
        far_all(j).wait_recv()
        mine = s3[j, xlo] + far_in[j, 0]
        other = far_in[j, 1] + far_in[j, 2]
        out_ref[:, columns(j)] = 0.5 * (other + sign * mine)

    lag = 1 if relay else 0

    def step(t, _):
        for stage, delay in ((after_core, 1), (after_y, 2), (after_z, 3), (after_far, 4)):
            j = t - lag - delay

            @pl.when((j >= 0) & (j < chunks))
            def _(stage=stage, j=j):
                stage(j)

        if relay:

            @pl.when(t < chunks)
            def _():
                relay_step(t)

        @pl.when((t >= lag) & (t - lag < chunks))
        def _():
            multiply(t - lag)

        return 0

    lax.fori_loop(0, chunks + lag + 4, step, 0)

    def drain(j, _):
        if relay:
            for way, peer in ways:
                own(j, way, peer).wait_send()
                forward(j, way, peer).wait_send()
        else:
            direct(j).wait_send()
        core_copy(j, 0, groups).wait_send()
        y_all(j).wait_send()
        z_all(j).wait_send()
        far_all(j).wait_send()
        return 0

    lax.fori_loop(0, chunks, drain, 0)


def shards(relay, tiles, trial):
    matrix, block = tiles[0], trial[0]
    width, depth = matrix.shape
    n = block.shape[1]
    n_z, n_y = lax.axis_size("z"), lax.axis_size("y")
    owners = lax.axis_size(OWNERS)
    rows = width // owners
    chunks = n // LANES
    groups = owners // (2 * n_y)
    f32, bf16 = jnp.float32, jnp.bfloat16
    dma = pltpu.SemaphoreType.DMA
    result = pl.pallas_call(
        functools.partial(kernel, n_z, n_y, rows, relay),
        out_shape=jax.ShapeDtypeStruct((rows, n), f32),
        in_specs=[pl.BlockSpec(memory_space=pl.ANY)] * 2,
        out_specs=pl.BlockSpec(memory_space=pltpu.VMEM),
        scratch_shapes=[
            pltpu.VMEM((chunks, depth, LANES), f32),
            pltpu.VMEM((chunks, depth, LANES), f32),
            pltpu.VMEM((chunks, 2, depth // 2, LANES), f32),
            pltpu.VMEM((width, depth), bf16),
            pltpu.VMEM((width, depth), bf16),
            pltpu.VMEM((2, STAGED, depth), f32),
            pltpu.VMEM((depth, 2 * LANES), bf16),
            pltpu.VMEM((chunks, groups, 2, n_y, rows, LANES), f32),
            pltpu.VMEM((chunks, groups, n_y, rows, LANES), f32),
            pltpu.VMEM((chunks, n_y - 1, groups, rows, LANES), f32),
            pltpu.VMEM((chunks, 2, n_z, rows, LANES), f32),
            pltpu.VMEM((chunks, n_z - 1, 2, rows, LANES), f32),
            pltpu.VMEM((chunks, 2, rows, LANES), f32),
            pltpu.VMEM((chunks, 3, rows, LANES), f32),
            dma((chunks,)),
            dma((2,)),
            *[dma((chunks, 2))] * 4,
            *[dma((chunks,))] * 8,
        ],
        compiler_params=pltpu.CompilerParams(
            collective_id=0, has_side_effects=True, vmem_limit_bytes=60 * 2**20
        ),
    )(matrix, block)
    return result[None]


RELAY = True


def solution(mesh):
    blk = mesh.shape["blk"]
    split = Mesh(
        mesh.devices.reshape(mesh.shape["pair"], 2, blk // 4, 2, mesh.shape["rows"]),
        AXES,
    )
    return jax.shard_map(
        functools.partial(shards, RELAY),
        mesh=split,
        in_specs=(P("pair", None, OWNERS), P("pair", OWNERS, None)),
        out_specs=P("pair", OWNERS, None),
        check_vma=False,
    )
```

```python
import functools

import jax
import jax.numpy as jnp
from jax import lax
from jax.experimental import pallas as pl
from jax.experimental.pallas import tpu as pltpu
from jax.sharding import Mesh
from jax.sharding import PartitionSpec as P

MESH = pl.DeviceIdType.MESH
AXES = ("pair", "xlo", "z", "core", "y")
OWNERS = ("xlo", "z", "core", "y")
LANES = 128
ROWS_AT_ONCE = 512
STAGED = 256


class Part:
    def __init__(self, at, refs):
        names = (
            "prod", "core_in", "y_in", "s2", "z_in", "s3", "far_in",
            "core_send", "core_recv", "y_send", "y_recv", "z_send", "z_recv", "far_send", "far_recv",
        )
        for name, ref in zip(names, refs):
            setattr(self, name, ref.at[at])


def kernel(n_z, n_y, rows, a_hbm, x_hbm, out_ref, *scratch):
    (xv, yv, xt, yt, a_hi, a_lo, staged, b_parts, acc) = scratch[:9]
    full, last = scratch[9:16], scratch[16:23]
    x_sem, a_sem, full_send, full_recv, last_send, last_recv = scratch[23:29]
    full, last = full + scratch[29:37], last + scratch[37:45]

    p, xlo, z, core, y = (lax.axis_index(a) for a in AXES)
    chunks = yv.shape[0]
    depth, width = a_hbm.shape[1], a_hbm.shape[0]
    half = depth // 2
    fine = xt.shape[2]
    sign = 1.0 - 2.0 * p.astype(jnp.float32)

    partner = {"pair": 1 - p}
    sibling = {"core": 1 - core}
    y_peers = [{"y": lax.rem(y + d, n_y)} for d in range(1, n_y)]
    z_peers = [{"z": lax.rem(z + d, n_z)} for d in range(1, n_z)]
    far_peers = [
        {"xlo": 1 - xlo},
        {"pair": 1 - p},
        {"pair": 1 - p, "xlo": 1 - xlo},
    ]
    peers = [sibling, *y_peers, *z_peers, *far_peers]

    barrier = pltpu.get_barrier_semaphore()
    for peer in peers:
        pl.semaphore_signal(barrier, inc=1, device_id=peer, device_id_type=MESH)

    def columns(j):
        return pl.ds(pl.multiple_of(j * LANES, LANES), LANES)

    def x_load(j):
        return pltpu.make_async_copy(x_hbm.at[:, columns(j)], xv.at[j], x_sem.at[j])

    def a_load(i):
        slot = lax.rem(i, 2)
        return pltpu.make_async_copy(
            a_hbm.at[pl.ds(pl.multiple_of(i * STAGED, STAGED), STAGED)], staged.at[slot], a_sem.at[slot]
        )

    def remote(src, dst, send, recv, peer):
        return pltpu.make_async_remote_copy(
            src_ref=src, dst_ref=dst, send_sem=send, recv_sem=recv, device_id=peer, device_id_type=MESH
        )

    def exchange(j, q):
        here = pl.ds(q * half, half)
        return remote(x_hbm.at[here, columns(j)], yv.at[j, here], full_send.at[j, q], full_recv.at[j, q], partner)

    def exchange_last(h):
        return remote(xt.at[h], yt.at[h], last_send.at[h], last_recv.at[h], partner)

    a_load(0).start()
    a_load(1).start()
    pl.semaphore_wait(barrier, len(peers))

    for q in range(2):
        exchange(0, q).start()

    def start_x(j, _):
        x_load(j).start()
        return 0

    lax.fori_loop(0, chunks + 1, start_x, 0)

    pieces = width // STAGED

    def split_a(i, _):
        a_load(i).wait()
        slot = lax.rem(i, 2)
        here = pl.ds(pl.multiple_of(i * STAGED, STAGED), STAGED)
        value = staged[slot]
        high = value.astype(jnp.bfloat16)
        a_hi[here] = high
        a_lo[here] = (value - high.astype(jnp.float32)).astype(jnp.bfloat16)

        @pl.when(i + 2 < pieces)
        def _():
            a_load(i + 2).start()

        return 0

    lax.fori_loop(0, pieces, split_a, 0)

    def turned(value):
        return pltpu.roll(value, LANES // 2, 1)

    def lower_half(shape):
        return lax.broadcasted_iota(jnp.int32, shape, len(shape) - 1) < LANES // 2

    x_load(chunks).wait()
    narrow = lower_half((fine, LANES))
    for b in range(4):
        upper = xv[chunks, pl.ds(2 * b * fine, fine)]
        lower = xv[chunks, pl.ds((2 * b + 1) * fine, fine)]
        xt[0, b] = jnp.where(narrow, upper, turned(lower))
        xt[1, b] = jnp.where(narrow, turned(upper), lower)

    groups = full[0].shape[1]
    blocks = width // ROWS_AT_ONCE
    step_groups = groups // blocks

    def core_copy(r, m):
        part = pl.ds(m * step_groups, step_groups)
        return remote(r.prod.at[part, 1 - core], r.core_in.at[part], r.core_send.at[m], r.core_recv.at[m], sibling)

    def multiply(j, q):
        exchange(j, q).wait_recv()
        later = j + 1 < chunks

        @pl.when(later)
        def _():
            exchange(j + 1, q).start()

        @pl.when(jnp.logical_not(later))
        def _():
            exchange_last(q).start()

        ks = pl.ds(q * half, half)
        combined = yv[j, ks] + sign * xv[j, ks]
        high = combined.astype(jnp.bfloat16)
        b_parts[ks, :LANES] = high
        b_parts[ks, LANES:] = (combined - high.astype(jnp.float32)).astype(jnp.bfloat16)
        r = Part(j, full)

        def rows_step(m, _):
            here = pl.ds(pl.multiple_of(m * ROWS_AT_ONCE, ROWS_AT_ONCE), ROWS_AT_ONCE)
            main = jnp.dot(a_hi[here, ks], b_parts[ks], preferred_element_type=jnp.float32)
            rest = jnp.dot(a_lo[here, ks], b_parts[ks, :LANES], preferred_element_type=jnp.float32)
            total = main[:, :LANES] + (main[:, LANES:] + rest)
            if q == 0:
                acc[here] = total
            else:
                total = total + acc[here]
                r.prod[pl.ds(m * step_groups, step_groups)] = total.reshape(step_groups, 2, n_y, rows, LANES)
                core_copy(r, m).start()
            return 0

        lax.fori_loop(0, blocks, rows_step, 0)

    def prepare_last(h):
        exchange_last(h).wait_recv()
        for b in range(4):
            combined = yt[h, b] + sign * xt[h, b]
            high = combined.astype(jnp.bfloat16).astype(jnp.float32)
            low = combined - high
            high_t, low_t = turned(high), turned(low)
            upper = pl.ds(2 * b * fine, fine)
            lower = pl.ds((2 * b + 1) * fine, fine)
            b_parts[upper, :LANES] = jnp.where(narrow, high, low_t).astype(jnp.bfloat16)
            b_parts[upper, LANES:] = jnp.where(narrow, high, high_t).astype(jnp.bfloat16)
            b_parts[lower, :LANES] = jnp.where(narrow, high_t, low).astype(jnp.bfloat16)
            b_parts[lower, LANES:] = jnp.where(narrow, high_t, high).astype(jnp.bfloat16)

    def multiply_last(r, m):
        here = pl.ds(pl.multiple_of(m * ROWS_AT_ONCE, ROWS_AT_ONCE), ROWS_AT_ONCE)
        main = jnp.dot(a_hi[here], b_parts[:, :LANES], preferred_element_type=jnp.float32)
        rest = jnp.dot(a_lo[here], b_parts[:, LANES:], preferred_element_type=jnp.float32)
        total = main + (turned(main) + rest)
        total = total.reshape(step_groups, 2, n_y, 2, rows // 2, LANES)
        packed = jnp.where(lower_half((step_groups, 2, n_y, rows // 2, LANES)), total[:, :, :, 0], total[:, :, :, 1])
        r.prod[pl.ds(m * step_groups, step_groups)] = packed
        core_copy(r, m).start()

    def y_copy(r, part, d):
        src = r.prod.at[part, core, lax.rem(y + d, n_y)]
        return remote(src, r.y_in.at[n_y - 1 - d, part], r.y_send, r.y_recv, y_peers[d - 1])

    def y_all(r):
        return remote(r.y_in, r.y_in, r.y_send, r.y_recv, y_peers[0])

    def z_copy(r, d):
        return remote(r.s2.at[:, lax.rem(z + d, n_z)], r.z_in.at[n_z - 1 - d], r.z_send, r.z_recv, z_peers[d - 1])

    def z_all(r):
        return remote(r.z_in, r.z_in, r.z_send, r.z_recv, z_peers[0])

    def far_copy(r, k):
        column = 1 - xlo if k != 1 else xlo
        return remote(r.s3.at[column], r.far_in.at[k], r.far_send, r.far_recv, far_peers[k])

    def far_all(r):
        return remote(r.far_in, r.far_in, r.far_send, r.far_recv, far_peers[0])

    def after_core(r, first=0, count=blocks):
        for m in range(first, first + count):
            core_copy(r, m).wait_recv()
        part = pl.ds(first * step_groups, count * step_groups)
        r.prod[part, core] = r.prod[part, core] + r.core_in[part]
        for d in range(1, n_y):
            y_copy(r, part, d).start()

    def after_y(r):
        y_all(r).wait_recv()
        total = r.prod[:, core, y]
        for d in range(n_y - 1):
            total = total + r.y_in[d]
        r.s2[...] = total.reshape(r.s2.shape)
        for d in range(1, n_z):
            z_copy(r, d).start()

    def after_z(r):
        z_all(r).wait_recv()
        total = r.s2[:, z]
        for d in range(n_z - 1):
            total = total + r.z_in[d]
        r.s3[...] = total
        for k in range(3):
            far_copy(r, k).start()

    def after_far(r):
        far_all(r).wait_recv()
        mine = r.s3[xlo] + r.far_in[0]
        other = r.far_in[1] + r.far_in[2]
        return 0.5 * (other + sign * mine)

    def finish(j):
        out_ref[:, columns(j)] = after_far(Part(j, full))

    def step(j, _):
        @pl.when(j >= 1)
        def _():
            after_core(Part(j - 1, full))

        x_load(j).wait()
        multiply(j, 0)
        for stage, delay in ((after_y, 2), (after_z, 3)):

            @pl.when(j >= delay)
            def _(stage=stage, at=j - delay):
                stage(Part(at, full))

        @pl.when(j >= 4)
        def _():
            finish(j - 4)

        multiply(j, 1)
        return 0

    lax.fori_loop(0, chunks, step, 0)

    f = [Part(j, full) for j in range(chunks)]
    e = [Part(h, last) for h in range(2)]
    n = chunks
    after_core(f[n - 1])
    after_y(f[n - 2])
    after_z(f[n - 3])
    finish(n - 4)
    prepare_last(0)

    def rows_step(m, _):
        multiply_last(e[0], m)
        return 0

    lax.fori_loop(0, blocks, rows_step, 0)
    prepare_last(1)
    multiply_last(e[1], 0)
    after_core(e[0])
    multiply_last(e[1], 1)
    after_core(e[1], 0, 1)
    after_y(f[n - 1])
    multiply_last(e[1], 2)
    after_core(e[1], 1, 1)
    multiply_last(e[1], 3)
    after_core(e[1], 2, 1)
    after_z(f[n - 2])
    finish(n - 3)
    after_core(e[1], 3, 1)
    after_y(e[0])
    after_y(e[1])
    after_z(f[n - 1])
    after_z(e[0])
    finish(n - 2)
    after_z(e[1])
    finish(n - 1)
    first_half, second_half = after_far(e[0]), after_far(e[1])
    narrow = lower_half((rows // 2, LANES))
    at = pl.ds(n * LANES, LANES)
    out_ref[: rows // 2, at] = jnp.where(narrow, first_half, turned(second_half))
    out_ref[rows // 2 :, at] = jnp.where(narrow, turned(first_half), second_half)

    def sent(r):
        for m in range(blocks):
            core_copy(r, m).wait_send()
        y_all(r).wait_send()
        z_all(r).wait_send()
        far_all(r).wait_send()

    def drain(j, _):
        for q in range(2):
            exchange(j, q).wait_send()
        sent(Part(j, full))
        return 0

    lax.fori_loop(0, chunks, drain, 0)
    for h in range(2):
        exchange_last(h).wait_send()
    for h in range(2):
        sent(e[h])


def shards(tiles, trial):
    matrix, block = tiles[0], trial[0]
    width, depth = matrix.shape
    n = block.shape[1]
    n_z, n_y = lax.axis_size("z"), lax.axis_size("y")
    owners = lax.axis_size(OWNERS)
    rows = width // owners
    chunks = n // LANES - 1
    groups = owners // (2 * n_y)
    fine = depth // 8
    f32, bf16 = jnp.float32, jnp.bfloat16
    dma = pltpu.SemaphoreType.DMA

    def reduction(count, height):
        return [
            pltpu.VMEM((count, groups, 2, n_y, height, LANES), f32),
            pltpu.VMEM((count, groups, n_y, height, LANES), f32),
            pltpu.VMEM((count, n_y - 1, groups, height, LANES), f32),
            pltpu.VMEM((count, 2, n_z, height, LANES), f32),
            pltpu.VMEM((count, n_z - 1, 2, height, LANES), f32),
            pltpu.VMEM((count, 2, height, LANES), f32),
            pltpu.VMEM((count, 3, height, LANES), f32),
        ]

    result = pl.pallas_call(
        functools.partial(kernel, n_z, n_y, rows),
        out_shape=jax.ShapeDtypeStruct((rows, n), f32),
        in_specs=[pl.BlockSpec(memory_space=pl.ANY)] * 2,
        out_specs=pl.BlockSpec(memory_space=pltpu.VMEM),
        scratch_shapes=[
            pltpu.VMEM((chunks + 1, depth, LANES), f32),
            pltpu.VMEM((chunks, depth, LANES), f32),
            *[pltpu.VMEM((2, 4, fine, LANES), f32)] * 2,
            pltpu.VMEM((width, depth), bf16),
            pltpu.VMEM((width, depth), bf16),
            pltpu.VMEM((2, STAGED, depth), f32),
            pltpu.VMEM((depth, 2 * LANES), bf16),
            pltpu.VMEM((width, LANES), f32),
            *reduction(chunks, rows),
            *reduction(2, rows // 2),
            dma((chunks + 1,)),
            dma((2,)),
            *[dma((chunks, 2))] * 2,
            *[dma((2,))] * 2,
            *[dma((chunks, width // ROWS_AT_ONCE))] * 2,
            *[dma((chunks,))] * 6,
            *[dma((2, width // ROWS_AT_ONCE))] * 2,
            *[dma((2,))] * 6,
        ],
        compiler_params=pltpu.CompilerParams(
            collective_id=0, has_side_effects=True, vmem_limit_bytes=60 * 2**20
        ),
    )(matrix, block)
    return result[None]


def solution(mesh):
    blk = mesh.shape["blk"]
    split = Mesh(
        mesh.devices.reshape(mesh.shape["pair"], 2, blk // 4, 2, mesh.shape["rows"]),
        AXES,
    )
    return jax.shard_map(
        shards,
        mesh=split,
        in_specs=(P("pair", None, OWNERS), P("pair", OWNERS, None)),
        out_specs=P("pair", OWNERS, None),
        check_vma=False,
    )
```

```python
import functools

import jax
import jax.numpy as jnp
from jax import lax
from jax.experimental import pallas as pl
from jax.experimental.pallas import tpu as pltpu
from jax.sharding import Mesh
from jax.sharding import PartitionSpec as P

MESH = pl.DeviceIdType.MESH
AXES = ("pair", "xlo", "z", "core", "y")
OWNERS = ("xlo", "z", "core", "y")
LANES = 128
ROWS_AT_ONCE = 512
STAGED = 256


class Part:
    def __init__(self, at, refs):
        names = (
            "prod", "core_in", "y_in", "s2", "z_in", "s3", "far_in",
            "core_send", "core_recv", "y_send", "y_recv", "z_send", "z_recv", "far_send", "far_recv",
        )
        for name, ref in zip(names, refs):
            setattr(self, name, ref.at[at])


def kernel(n_z, n_y, rows, a_hbm, x_hbm, out_ref, *scratch):
    (xv, yv, xt, yt, a_hi, a_lo, staged, b_parts, acc) = scratch[:9]
    full, last = scratch[9:16], scratch[16:23]
    x_sem, a_sem, full_send, full_recv, last_send, last_recv = scratch[23:29]
    full, last = full + scratch[29:37], last + scratch[37:45]

    p, xlo, z, core, y = (lax.axis_index(a) for a in AXES)
    chunks = yv.shape[0]
    depth, width = a_hbm.shape[1], a_hbm.shape[0]
    half = depth // 2
    fine = xt.shape[2]
    sign = 1.0 - 2.0 * p.astype(jnp.float32)

    partner = {"pair": 1 - p}
    sibling = {"core": 1 - core}
    y_peers = [{"y": lax.rem(y + d, n_y)} for d in range(1, n_y)]
    z_peers = [{"z": lax.rem(z + d, n_z)} for d in range(1, n_z)]
    far_peers = [
        {"xlo": 1 - xlo},
        {"pair": 1 - p},
        {"pair": 1 - p, "xlo": 1 - xlo},
    ]
    peers = [sibling, *y_peers, *z_peers, *far_peers]

    barrier = pltpu.get_barrier_semaphore()
    for peer in peers:
        pl.semaphore_signal(barrier, inc=1, device_id=peer, device_id_type=MESH)

    def columns(j):
        return pl.ds(pl.multiple_of(j * LANES, LANES), LANES)

    def x_load(j):
        return pltpu.make_async_copy(x_hbm.at[:, columns(j)], xv.at[j], x_sem.at[j])

    def a_load(i):
        slot = lax.rem(i, 2)
        return pltpu.make_async_copy(
            a_hbm.at[pl.ds(pl.multiple_of(i * STAGED, STAGED), STAGED)], staged.at[slot], a_sem.at[slot]
        )

    def remote(src, dst, send, recv, peer):
        return pltpu.make_async_remote_copy(
            src_ref=src, dst_ref=dst, send_sem=send, recv_sem=recv, device_id=peer, device_id_type=MESH
        )

    def exchange(j, q):
        here = pl.ds(q * half, half)
        return remote(x_hbm.at[here, columns(j)], yv.at[j, here], full_send.at[j, q], full_recv.at[j, q], partner)

    def exchange_last(h):
        return remote(xt.at[h], yt.at[h], last_send.at[h], last_recv.at[h], partner)

    a_load(0).start()
    a_load(1).start()
    pl.semaphore_wait(barrier, len(peers))

    for q in range(2):
        exchange(0, q).start()

    def start_x(j, _):
        x_load(j).start()
        return 0

    lax.fori_loop(0, chunks + 1, start_x, 0)

    pieces = width // STAGED

    def split_a(i, _):
        a_load(i).wait()
        slot = lax.rem(i, 2)
        here = pl.ds(pl.multiple_of(i * STAGED, STAGED), STAGED)
        value = staged[slot]
        high = value.astype(jnp.bfloat16)
        a_hi[here] = high
        a_lo[here] = (value - high.astype(jnp.float32)).astype(jnp.bfloat16)

        @pl.when(i + 2 < pieces)
        def _():
            a_load(i + 2).start()

        return 0

    lax.fori_loop(0, pieces, split_a, 0)

    def turned(value):
        return pltpu.roll(value, LANES // 2, 1)

    def lower_half(shape):
        return lax.broadcasted_iota(jnp.int32, shape, len(shape) - 1) < LANES // 2

    x_load(chunks).wait()
    narrow = lower_half((fine, LANES))
    for b in range(4):
        upper = xv[chunks, pl.ds(2 * b * fine, fine)]
        lower = xv[chunks, pl.ds((2 * b + 1) * fine, fine)]
        xt[0, b] = jnp.where(narrow, upper, turned(lower))
        xt[1, b] = jnp.where(narrow, turned(upper), lower)

    groups = full[0].shape[1]
    blocks = width // ROWS_AT_ONCE
    step_groups = groups // blocks

    def core_copy(r, m):
        part = pl.ds(m * step_groups, step_groups)
        return remote(r.prod.at[part, 1 - core], r.core_in.at[part], r.core_send.at[m], r.core_recv.at[m], sibling)

    def multiply(j, q):
        exchange(j, q).wait_recv()
        later = j + 1 < chunks

        @pl.when(later)
        def _():
            exchange(j + 1, q).start()

        @pl.when(jnp.logical_not(later))
        def _():
            exchange_last(q).start()

        ks = pl.ds(q * half, half)
        combined = yv[j, ks] + sign * xv[j, ks]
        high = combined.astype(jnp.bfloat16)
        b_parts[ks, :LANES] = high
        b_parts[ks, LANES:] = (combined - high.astype(jnp.float32)).astype(jnp.bfloat16)
        r = Part(j, full)

        def rows_step(m, _):
            here = pl.ds(pl.multiple_of(m * ROWS_AT_ONCE, ROWS_AT_ONCE), ROWS_AT_ONCE)
            main = jnp.dot(a_hi[here, ks], b_parts[ks], preferred_element_type=jnp.float32)
            rest = jnp.dot(a_lo[here, ks], b_parts[ks, :LANES], preferred_element_type=jnp.float32)
            total = main[:, :LANES] + (main[:, LANES:] + rest)
            if q == 0:
                acc[here] = total
            else:
                total = total + acc[here]
                r.prod[pl.ds(m * step_groups, step_groups)] = total.reshape(step_groups, 2, n_y, rows, LANES)
                core_copy(r, m).start()
            return 0

        lax.fori_loop(0, blocks, rows_step, 0)

    def prepare_last(h):
        exchange_last(h).wait_recv()
        for b in range(4):
            combined = yt[h, b] + sign * xt[h, b]
            high = combined.astype(jnp.bfloat16).astype(jnp.float32)
            low = combined - high
            high_t, low_t = turned(high), turned(low)
            upper = pl.ds(2 * b * fine, fine)
            lower = pl.ds((2 * b + 1) * fine, fine)
            b_parts[upper, :LANES] = jnp.where(narrow, high, low_t).astype(jnp.bfloat16)
            b_parts[upper, LANES:] = jnp.where(narrow, high, high_t).astype(jnp.bfloat16)
            b_parts[lower, :LANES] = jnp.where(narrow, high_t, low).astype(jnp.bfloat16)
            b_parts[lower, LANES:] = jnp.where(narrow, high_t, high).astype(jnp.bfloat16)

    def multiply_last(r, m):
        here = pl.ds(pl.multiple_of(m * ROWS_AT_ONCE, ROWS_AT_ONCE), ROWS_AT_ONCE)
        main = jnp.dot(a_hi[here], b_parts[:, :LANES], preferred_element_type=jnp.float32)
        rest = jnp.dot(a_lo[here], b_parts[:, LANES:], preferred_element_type=jnp.float32)
        total = main + (turned(main) + rest)
        total = total.reshape(step_groups, 2, n_y, 2, rows // 2, LANES)
        packed = jnp.where(lower_half((step_groups, 2, n_y, rows // 2, LANES)), total[:, :, :, 0], total[:, :, :, 1])
        r.prod[pl.ds(m * step_groups, step_groups)] = packed
        core_copy(r, m).start()

    def y_copy(r, part, d):
        src = r.prod.at[part, core, lax.rem(y + d, n_y)]
        return remote(src, r.y_in.at[n_y - 1 - d, part], r.y_send, r.y_recv, y_peers[d - 1])

    def y_all(r):
        return remote(r.y_in, r.y_in, r.y_send, r.y_recv, y_peers[0])

    def z_copy(r, d):
        return remote(r.s2.at[:, lax.rem(z + d, n_z)], r.z_in.at[n_z - 1 - d], r.z_send, r.z_recv, z_peers[d - 1])

    def z_all(r):
        return remote(r.z_in, r.z_in, r.z_send, r.z_recv, z_peers[0])

    def far_copy(r, k):
        column = 1 - xlo if k != 1 else xlo
        return remote(r.s3.at[column], r.far_in.at[k], r.far_send, r.far_recv, far_peers[k])

    def far_all(r):
        return remote(r.far_in, r.far_in, r.far_send, r.far_recv, far_peers[0])

    def after_core(r, first=0, count=blocks):
        for m in range(first, first + count):
            core_copy(r, m).wait_recv()
        part = pl.ds(first * step_groups, count * step_groups)
        r.prod[part, core] = r.prod[part, core] + r.core_in[part]
        for d in range(1, n_y):
            y_copy(r, part, d).start()

    def after_y(r):
        y_all(r).wait_recv()
        total = r.prod[:, core, y]
        for d in range(n_y - 1):
            total = total + r.y_in[d]
        r.s2[...] = total.reshape(r.s2.shape)
        for d in range(1, n_z):
            z_copy(r, d).start()

    def sum_z(r):
        z_all(r).wait_recv()
        total = r.s2[:, z]
        for d in range(n_z - 1):
            total = total + r.z_in[d]
        r.s3[...] = total

    def send_far(r):
        for k in range(3):
            far_copy(r, k).start()

    def after_z(r):
        sum_z(r)
        send_far(r)

    def after_far(r):
        far_all(r).wait_recv()
        mine = r.s3[xlo] + r.far_in[0]
        other = r.far_in[1] + r.far_in[2]
        return 0.5 * (other + sign * mine)

    def finish(j):
        out_ref[:, columns(j)] = after_far(Part(j, full))

    def step(j, _):
        @pl.when(j >= 1)
        def _():
            after_core(Part(j - 1, full))

        x_load(j).wait()
        multiply(j, 0)
        for stage, delay in ((after_y, 2), (sum_z, 3)):

            @pl.when(j >= delay)
            def _(stage=stage, at=j - delay):
                stage(Part(at, full))

        multiply(j, 1)
        return 0

    def sent(r):
        for m in range(blocks):
            core_copy(r, m).wait_send()
        y_all(r).wait_send()

    lax.fori_loop(0, chunks, step, 0)

    f = [Part(j, full) for j in range(chunks)]
    e = [Part(h, last) for h in range(2)]
    n = chunks
    after_core(f[n - 1])
    after_y(f[n - 2])
    sum_z(f[n - 3])
    prepare_last(0)

    def early_far(j, _):
        send_far(Part(j, full))
        return 0

    def early_finish(j, _):
        finish(j)
        return 0

    multiply_last(e[0], 0)
    multiply_last(e[0], 1)
    after_core(e[0], 0, 1)
    multiply_last(e[0], 2)
    after_core(e[0], 1, 1)
    multiply_last(e[0], 3)
    after_core(e[0], 2, 1)
    prepare_last(1)
    multiply_last(e[1], 0)
    after_core(e[0], 3, 1)
    multiply_last(e[1], 1)
    after_core(e[1], 0, 1)
    multiply_last(e[1], 2)
    after_core(e[1], 1, 1)
    multiply_last(e[1], 3)
    after_core(e[1], 2, 1)
    after_y(f[n - 1])
    after_core(e[1], 3, 1)
    after_y(e[0])
    after_z(f[n - 2])
    lax.fori_loop(0, n - 2, early_far, 0)
    after_y(e[1])
    lax.fori_loop(0, n - 2, early_finish, 0)
    after_z(f[n - 1])
    after_z(e[0])

    def drain(j, _):
        for q in range(2):
            exchange(j, q).wait_send()
        r = Part(j, full)
        sent(r)
        z_all(r).wait_send()
        return 0

    lax.fori_loop(0, chunks, drain, 0)
    for h in range(2):
        exchange_last(h).wait_send()
        sent(e[h])
    z_all(e[0]).wait_send()
    after_z(e[1])
    finish(n - 2)
    finish(n - 1)

    def drain_far(j, _):
        far_all(Part(j, full)).wait_send()
        return 0

    lax.fori_loop(0, chunks, drain_far, 0)
    far_all(e[0]).wait_send()
    z_all(e[1]).wait_send()
    first_half = after_far(e[0])
    second_half = after_far(e[1])
    narrow = lower_half((rows // 2, LANES))
    at = pl.ds(n * LANES, LANES)
    out_ref[: rows // 2, at] = jnp.where(narrow, first_half, turned(second_half))
    out_ref[rows // 2 :, at] = jnp.where(narrow, turned(first_half), second_half)
    far_all(e[1]).wait_send()


def shards(tiles, trial):
    matrix, block = tiles[0], trial[0]
    width, depth = matrix.shape
    n = block.shape[1]
    n_z, n_y = lax.axis_size("z"), lax.axis_size("y")
    owners = lax.axis_size(OWNERS)
    rows = width // owners
    chunks = n // LANES - 1
    groups = owners // (2 * n_y)
    fine = depth // 8
    f32, bf16 = jnp.float32, jnp.bfloat16
    dma = pltpu.SemaphoreType.DMA

    def reduction(count, height):
        return [
            pltpu.VMEM((count, groups, 2, n_y, height, LANES), f32),
            pltpu.VMEM((count, groups, n_y, height, LANES), f32),
            pltpu.VMEM((count, n_y - 1, groups, height, LANES), f32),
            pltpu.VMEM((count, 2, n_z, height, LANES), f32),
            pltpu.VMEM((count, n_z - 1, 2, height, LANES), f32),
            pltpu.VMEM((count, 2, height, LANES), f32),
            pltpu.VMEM((count, 3, height, LANES), f32),
        ]

    result = pl.pallas_call(
        functools.partial(kernel, n_z, n_y, rows),
        out_shape=pltpu.VMEM((rows, n), f32),
        in_specs=[pl.BlockSpec(memory_space=pl.ANY)] * 2,
        out_specs=pl.BlockSpec(memory_space=pltpu.VMEM),
        scratch_shapes=[
            pltpu.VMEM((chunks + 1, depth, LANES), f32),
            pltpu.VMEM((chunks, depth, LANES), f32),
            *[pltpu.VMEM((2, 4, fine, LANES), f32)] * 2,
            pltpu.VMEM((width, depth), bf16),
            pltpu.VMEM((width, depth), bf16),
            pltpu.VMEM((2, STAGED, depth), f32),
            pltpu.VMEM((depth, 2 * LANES), bf16),
            pltpu.VMEM((width, LANES), f32),
            *reduction(chunks, rows),
            *reduction(2, rows // 2),
            dma((chunks + 1,)),
            dma((2,)),
            *[dma((chunks, 2))] * 2,
            *[dma((2,))] * 2,
            *[dma((chunks, width // ROWS_AT_ONCE))] * 2,
            *[dma((chunks,))] * 6,
            *[dma((2, width // ROWS_AT_ONCE))] * 2,
            *[dma((2,))] * 6,
        ],
        compiler_params=pltpu.CompilerParams(
            collective_id=0, has_side_effects=True, vmem_limit_bytes=60 * 2**20
        ),
    )(matrix, block)
    return result[None]


def solution(mesh):
    blk = mesh.shape["blk"]
    split = Mesh(
        mesh.devices.reshape(mesh.shape["pair"], 2, blk // 4, 2, mesh.shape["rows"]),
        AXES,
    )
    return jax.shard_map(
        shards,
        mesh=split,
        in_specs=(P("pair", None, OWNERS), P("pair", OWNERS, None)),
        out_specs=P("pair", OWNERS, None),
        check_vma=False,
    )
```

```python
import functools

import jax
import jax.numpy as jnp
from jax import lax
from jax.experimental import pallas as pl
from jax.experimental.pallas import tpu as pltpu
from jax.sharding import Mesh
from jax.sharding import PartitionSpec as P

MESH = pl.DeviceIdType.MESH
AXES = ("pair", "xlo", "z", "core", "y")
OWNERS = ("xlo", "z", "core", "y")
LANES = 128
ROWS_AT_ONCE = 512
STAGED = 256


def farthest_first(n):
    return sorted(range(1, n), key=lambda d: -min(d, n - d))


class Part:
    def __init__(self, at, refs):
        names = (
            "prod", "core_in", "y_in", "s2", "z_in", "s3", "far_in",
            "core_send", "core_recv", "y_send", "y_recv", "z_send", "z_recv", "far_send", "far_recv",
        )
        for name, ref in zip(names, refs):
            setattr(self, name, ref.at[at])


def kernel(n_z, n_y, rows, a_hbm, x_hbm, out_ref, *scratch):
    (xv, yv, xt, yt, a_hi, a_lo, staged, b_parts, acc) = scratch[:9]
    full, last = scratch[9:16], scratch[16:23]
    x_sem, a_sem, full_send, full_recv, last_send, last_recv = scratch[23:29]
    full, last = full + scratch[29:37], last + scratch[37:45]

    p, xlo, z, core, y = (lax.axis_index(a) for a in AXES)
    chunks = yv.shape[0]
    depth, width = a_hbm.shape[1], a_hbm.shape[0]
    half = depth // 2
    fine = xt.shape[2]
    sign = 1.0 - 2.0 * p.astype(jnp.float32)

    partner = {"pair": 1 - p}
    sibling = {"core": 1 - core}
    y_peers = [{"y": lax.rem(y + d, n_y)} for d in range(1, n_y)]
    z_peers = [{"z": lax.rem(z + d, n_z)} for d in range(1, n_z)]
    far_peers = [
        {"xlo": 1 - xlo},
        {"pair": 1 - p},
        {"pair": 1 - p, "xlo": 1 - xlo},
    ]
    peers = [sibling, *y_peers, *z_peers, *far_peers]

    barrier = pltpu.get_barrier_semaphore()
    for peer in peers:
        pl.semaphore_signal(barrier, inc=1, device_id=peer, device_id_type=MESH)

    def columns(j):
        return pl.ds(pl.multiple_of(j * LANES, LANES), LANES)

    def x_load(j):
        return pltpu.make_async_copy(x_hbm.at[:, columns(j)], xv.at[j], x_sem.at[j])

    def a_load(i):
        slot = lax.rem(i, 2)
        return pltpu.make_async_copy(
            a_hbm.at[pl.ds(pl.multiple_of(i * STAGED, STAGED), STAGED)], staged.at[slot], a_sem.at[slot]
        )

    def remote(src, dst, send, recv, peer):
        return pltpu.make_async_remote_copy(
            src_ref=src, dst_ref=dst, send_sem=send, recv_sem=recv, device_id=peer, device_id_type=MESH
        )

    def exchange(j, q):
        here = pl.ds(q * half, half)
        return remote(x_hbm.at[here, columns(j)], yv.at[j, here], full_send.at[j, q], full_recv.at[j, q], partner)

    def exchange_last(h):
        return remote(xt.at[h], yt.at[h], last_send.at[h], last_recv.at[h], partner)

    a_load(0).start()
    a_load(1).start()
    pl.semaphore_wait(barrier, len(peers))

    for q in range(2):
        exchange(0, q).start()

    def start_x(j, _):
        x_load(j).start()
        return 0

    lax.fori_loop(0, chunks + 1, start_x, 0)

    pieces = width // STAGED

    def split_a(i, _):
        a_load(i).wait()
        slot = lax.rem(i, 2)
        here = pl.ds(pl.multiple_of(i * STAGED, STAGED), STAGED)
        value = staged[slot]
        high = value.astype(jnp.bfloat16)
        a_hi[here] = high
        a_lo[here] = (value - high.astype(jnp.float32)).astype(jnp.bfloat16)

        @pl.when(i + 2 < pieces)
        def _():
            a_load(i + 2).start()

        return 0

    lax.fori_loop(0, pieces, split_a, 0)

    def turned(value):
        return pltpu.roll(value, LANES // 2, 1)

    def lower_half(shape):
        return lax.broadcasted_iota(jnp.int32, shape, len(shape) - 1) < LANES // 2

    x_load(chunks).wait()
    narrow = lower_half((fine, LANES))
    for b in range(4):
        upper = xv[chunks, pl.ds(2 * b * fine, fine)]
        lower = xv[chunks, pl.ds((2 * b + 1) * fine, fine)]
        xt[0, b] = jnp.where(narrow, upper, turned(lower))
        xt[1, b] = jnp.where(narrow, turned(upper), lower)

    groups = full[0].shape[1]
    blocks = width // ROWS_AT_ONCE
    step_groups = groups // blocks

    def core_copy(r, m):
        part = pl.ds(m * step_groups, step_groups)
        return remote(r.prod.at[part, 1 - core], r.core_in.at[part], r.core_send.at[m], r.core_recv.at[m], sibling)

    def multiply(j, q):
        exchange(j, q).wait_recv()
        later = j + 1 < chunks

        @pl.when(later)
        def _():
            exchange(j + 1, q).start()

        @pl.when(jnp.logical_not(later))
        def _():
            exchange_last(q).start()

        ks = pl.ds(q * half, half)
        combined = yv[j, ks] + sign * xv[j, ks]
        high = combined.astype(jnp.bfloat16)
        b_parts[ks, :LANES] = high
        b_parts[ks, LANES:] = (combined - high.astype(jnp.float32)).astype(jnp.bfloat16)
        r = Part(j, full)

        def rows_step(m, _):
            here = pl.ds(pl.multiple_of(m * ROWS_AT_ONCE, ROWS_AT_ONCE), ROWS_AT_ONCE)
            main = jnp.dot(a_hi[here, ks], b_parts[ks], preferred_element_type=jnp.float32)
            rest = jnp.dot(a_lo[here, ks], b_parts[ks, :LANES], preferred_element_type=jnp.float32)
            total = main[:, :LANES] + (main[:, LANES:] + rest)
            if q == 0:
                acc[here] = total
            else:
                total = total + acc[here]
                r.prod[pl.ds(m * step_groups, step_groups)] = total.reshape(step_groups, 2, n_y, rows, LANES)
                core_copy(r, m).start()
            return 0

        lax.fori_loop(0, blocks, rows_step, 0)

    def prepare_last(h):
        exchange_last(h).wait_recv()
        for b in range(4):
            combined = yt[h, b] + sign * xt[h, b]
            high = combined.astype(jnp.bfloat16).astype(jnp.float32)
            low = combined - high
            high_t, low_t = turned(high), turned(low)
            upper = pl.ds(2 * b * fine, fine)
            lower = pl.ds((2 * b + 1) * fine, fine)
            b_parts[upper, :LANES] = jnp.where(narrow, high, low_t).astype(jnp.bfloat16)
            b_parts[upper, LANES:] = jnp.where(narrow, high, high_t).astype(jnp.bfloat16)
            b_parts[lower, :LANES] = jnp.where(narrow, high_t, low).astype(jnp.bfloat16)
            b_parts[lower, LANES:] = jnp.where(narrow, high_t, high).astype(jnp.bfloat16)

    def multiply_last(r, m):
        here = pl.ds(pl.multiple_of(m * ROWS_AT_ONCE, ROWS_AT_ONCE), ROWS_AT_ONCE)
        main = jnp.dot(a_hi[here], b_parts[:, :LANES], preferred_element_type=jnp.float32)
        rest = jnp.dot(a_lo[here], b_parts[:, LANES:], preferred_element_type=jnp.float32)
        total = main + (turned(main) + rest)
        total = total.reshape(step_groups, 2, n_y, 2, rows // 2, LANES)
        packed = jnp.where(lower_half((step_groups, 2, n_y, rows // 2, LANES)), total[:, :, :, 0], total[:, :, :, 1])
        r.prod[pl.ds(m * step_groups, step_groups)] = packed
        core_copy(r, m).start()

    def y_copy(r, part, d):
        src = r.prod.at[part, core, lax.rem(y + d, n_y)]
        return remote(src, r.y_in.at[n_y - 1 - d, part], r.y_send, r.y_recv, y_peers[d - 1])

    def y_all(r):
        return remote(r.y_in, r.y_in, r.y_send, r.y_recv, y_peers[0])

    def z_copy(r, d):
        return remote(r.s2.at[:, lax.rem(z + d, n_z)], r.z_in.at[n_z - 1 - d], r.z_send, r.z_recv, z_peers[d - 1])

    def z_all(r):
        return remote(r.z_in, r.z_in, r.z_send, r.z_recv, z_peers[0])

    def far_copy(r, k):
        column = 1 - xlo if k != 1 else xlo
        return remote(r.s3.at[column], r.far_in.at[k], r.far_send, r.far_recv, far_peers[k])

    def far_all(r):
        return remote(r.far_in, r.far_in, r.far_send, r.far_recv, far_peers[0])

    def after_core(r, first=0, count=blocks):
        for m in range(first, first + count):
            core_copy(r, m).wait_recv()
        part = pl.ds(first * step_groups, count * step_groups)
        r.prod[part, core] = r.prod[part, core] + r.core_in[part]
        for d in farthest_first(n_y):
            y_copy(r, part, d).start()

    def after_y(r):
        y_all(r).wait_recv()
        total = r.prod[:, core, y]
        for d in range(n_y - 1):
            total = total + r.y_in[d]
        r.s2[...] = total.reshape(r.s2.shape)
        for d in farthest_first(n_z):
            z_copy(r, d).start()

    def sum_z(r):
        z_all(r).wait_recv()
        total = r.s2[:, z]
        for d in range(n_z - 1):
            total = total + r.z_in[d]
        r.s3[...] = total

    def send_far(r):
        for k in (1, 0, 2):
            far_copy(r, k).start()

    def after_z(r):
        sum_z(r)
        send_far(r)

    def after_far(r):
        far_all(r).wait_recv()
        mine = r.s3[xlo] + r.far_in[0]
        other = r.far_in[1] + r.far_in[2]
        return 0.5 * (other + sign * mine)

    def finish(j):
        out_ref[:, columns(j)] = after_far(Part(j, full))

    def step(j, _):
        @pl.when(j >= 1)
        def _():
            after_core(Part(j - 1, full))

        x_load(j).wait()
        multiply(j, 0)
        for stage, delay in ((after_y, 2), (sum_z, 3)):

            @pl.when(j >= delay)
            def _(stage=stage, at=j - delay):
                stage(Part(at, full))

        multiply(j, 1)
        return 0

    def sent(r):
        for m in range(blocks):
            core_copy(r, m).wait_send()
        y_all(r).wait_send()

    lax.fori_loop(0, chunks, step, 0)

    f = [Part(j, full) for j in range(chunks)]
    e = [Part(h, last) for h in range(2)]
    n = chunks
    after_core(f[n - 1])
    after_y(f[n - 2])
    sum_z(f[n - 3])
    prepare_last(0)

    def early_far(j, _):
        send_far(Part(j, full))
        return 0

    def early_finish(j, _):
        finish(j)
        return 0

    multiply_last(e[0], 0)
    multiply_last(e[0], 1)
    after_core(e[0], 0, 1)
    multiply_last(e[0], 2)
    after_core(e[0], 1, 1)
    multiply_last(e[0], 3)
    after_core(e[0], 2, 1)
    prepare_last(1)
    multiply_last(e[1], 0)
    after_core(e[0], 3, 1)
    multiply_last(e[1], 1)
    after_core(e[1], 0, 1)
    multiply_last(e[1], 2)
    after_core(e[1], 1, 1)
    multiply_last(e[1], 3)
    after_core(e[1], 2, 1)
    after_y(f[n - 1])
    after_core(e[1], 3, 1)
    after_y(e[0])
    after_z(f[n - 2])
    lax.fori_loop(0, n - 2, early_far, 0)
    after_y(e[1])
    lax.fori_loop(0, n - 2, early_finish, 0)
    after_z(f[n - 1])
    after_z(e[0])

    def drain(j, _):
        for q in range(2):
            exchange(j, q).wait_send()
        r = Part(j, full)
        sent(r)
        z_all(r).wait_send()
        return 0

    lax.fori_loop(0, chunks, drain, 0)
    for h in range(2):
        exchange_last(h).wait_send()
        sent(e[h])
    z_all(e[0]).wait_send()
    after_z(e[1])
    finish(n - 2)
    finish(n - 1)

    def drain_far(j, _):
        far_all(Part(j, full)).wait_send()
        return 0

    lax.fori_loop(0, chunks, drain_far, 0)
    far_all(e[0]).wait_send()
    z_all(e[1]).wait_send()
    first_half = after_far(e[0])
    second_half = after_far(e[1])
    narrow = lower_half((rows // 2, LANES))
    at = pl.ds(n * LANES, LANES)
    out_ref[: rows // 2, at] = jnp.where(narrow, first_half, turned(second_half))
    out_ref[rows // 2 :, at] = jnp.where(narrow, turned(first_half), second_half)
    far_all(e[1]).wait_send()


def shards(tiles, trial):
    matrix, block = tiles[0], trial[0]
    width, depth = matrix.shape
    n = block.shape[1]
    n_z, n_y = lax.axis_size("z"), lax.axis_size("y")
    owners = lax.axis_size(OWNERS)
    rows = width // owners
    chunks = n // LANES - 1
    groups = owners // (2 * n_y)
    fine = depth // 8
    f32, bf16 = jnp.float32, jnp.bfloat16
    dma = pltpu.SemaphoreType.DMA

    def reduction(count, height):
        return [
            pltpu.VMEM((count, groups, 2, n_y, height, LANES), f32),
            pltpu.VMEM((count, groups, n_y, height, LANES), f32),
            pltpu.VMEM((count, n_y - 1, groups, height, LANES), f32),
            pltpu.VMEM((count, 2, n_z, height, LANES), f32),
            pltpu.VMEM((count, n_z - 1, 2, height, LANES), f32),
            pltpu.VMEM((count, 2, height, LANES), f32),
            pltpu.VMEM((count, 3, height, LANES), f32),
        ]

    result = pl.pallas_call(
        functools.partial(kernel, n_z, n_y, rows),
        out_shape=pltpu.VMEM((rows, n), f32),
        in_specs=[pl.BlockSpec(memory_space=pl.ANY)] * 2,
        out_specs=pl.BlockSpec(memory_space=pltpu.VMEM),
        scratch_shapes=[
            pltpu.VMEM((chunks + 1, depth, LANES), f32),
            pltpu.VMEM((chunks, depth, LANES), f32),
            *[pltpu.VMEM((2, 4, fine, LANES), f32)] * 2,
            pltpu.VMEM((width, depth), bf16),
            pltpu.VMEM((width, depth), bf16),
            pltpu.VMEM((2, STAGED, depth), f32),
            pltpu.VMEM((depth, 2 * LANES), bf16),
            pltpu.VMEM((width, LANES), f32),
            *reduction(chunks, rows),
            *reduction(2, rows // 2),
            dma((chunks + 1,)),
            dma((2,)),
            *[dma((chunks, 2))] * 2,
            *[dma((2,))] * 2,
            *[dma((chunks, width // ROWS_AT_ONCE))] * 2,
            *[dma((chunks,))] * 6,
            *[dma((2, width // ROWS_AT_ONCE))] * 2,
            *[dma((2,))] * 6,
        ],
        compiler_params=pltpu.CompilerParams(
            collective_id=0, has_side_effects=True, vmem_limit_bytes=60 * 2**20
        ),
    )(matrix, block)
    return result[None]


def solution(mesh):
    blk = mesh.shape["blk"]
    split = Mesh(
        mesh.devices.reshape(mesh.shape["pair"], 2, blk // 4, 2, mesh.shape["rows"]),
        AXES,
    )
    return jax.shard_map(
        shards,
        mesh=split,
        in_specs=(P("pair", None, OWNERS), P("pair", OWNERS, None)),
        out_specs=P("pair", OWNERS, None),
        check_vma=False,
    )
```
